32 devices in a mesh: seq: 8 (over y, x, core), layer: 4 (over z).
Axes of the slice: x: 2, y: 2, z: 4, core: 2. Of those that a mesh axis runs over, the one named last changes fastest.
Arguments:
- target_enc: bfloat16 [1024, 4096], P('seq'), may hold values from -1000 to 1000
- source_enc: bfloat16 [4, 1024, 4096], P('layer', 'seq'), may hold values from -1000 to 1000
- span_start: int32 [64], replicated, may hold values from 0 to 1015, as said below
- span_end: int32 [64], replicated, may hold values from 8 to 1024, as said below
- span_source: int32 [64], replicated, may hold values from 0 to 3
- norm_gain: float32 [4096], replicated, may hold values from 0.1 to 1.9
- w_key: bfloat16 [4, 4096, 2048], P('layer', None, 'seq'), may hold values from -0.09375 to 0.09375
- w_value: bfloat16 [4, 4096, 2048], P('layer', None, 'seq'), may hold values from -0.09375 to 0.09375
- queries: bfloat16 [4, 512, 2048], P('layer', None, 'seq'), may hold values from -14 to 14
- key_len: int32 [512], replicated, may hold values from 256 to 1024, as said below
Outputs:
- context: bfloat16 [4, 512, 2048], P('layer', None, 'seq')
The draws below stay inside these ranges and needn't reach their ends.
Inputs may be any that keep to these rules, and one draw needn't show every extreme that they name: `span_start`: span k lies inside the k-th of 64 equal segments of the tokens, starts in the first half of it and covers at least half of it; spans are disjoint and ordered. span_end[k] - span_start[k] is at least half a segment, and span_end[k] is at most the end of the k-th segment. `key_len`: some query token sees all 1024 encoder tokens.
All inputs are finite; a program needn't handle non-finite values.
Results may differ from the reference program's by a relative error of at most 0.003.
The reference program's roundings to bfloat16 on the way (of `patched`, `normed` and `probs`) count: a program that leaves them out, or rounds other values in their place, can miss the bound.
Values may be sent and summed in bfloat16 or wider, within the bound.
A program may use at most 64 MiB of HBM per device.

```python
import math
import jax
import jax.numpy as jnp
from jax import lax

D = 4096
HEAD = 256
HEADS = 8
HD = 2048
LAYERS = 4
TOKENS = 1024
QB = 512
SPANS = 64
SOURCES = 4


def span_pair(key):
    inner = jax.random.fold_in(key, 101)
    first, second = jax.random.split(inner)
    seglen = TOKENS // SPANS
    half = seglen // 2
    offsets = jax.random.randint(first, (SPANS,), 0, half)
    index = jnp.arange(SPANS, dtype=jnp.int32)
    offsets = jnp.where(index == 0, 0, offsets)
    offsets = jnp.where(index == SPANS - 1, half - 1, offsets)
    room = seglen - offsets
    widths = jax.random.randint(second, (SPANS,), half, room + 1)
    widths = jnp.where(index == 0, half, widths)
    widths = jnp.where(index == SPANS - 1, room, widths)
    starts = index * seglen + offsets
    return (starts.astype(jnp.int32), (starts + widths).astype(jnp.int32))


def draw_span_start(key, part):
    return span_pair(key)[0]


def draw_span_end(key, part):
    return span_pair(key)[1]


def draw_key_len(key, part):
    first, second = jax.random.split(jax.random.fold_in(key, 202))
    lengths = jax.random.randint(first, (QB,), TOKENS // 4, TOKENS + 1)
    chosen = jax.random.randint(second, (), 0, QB)
    return jnp.where(jnp.arange(QB) == chosen, TOKENS, lengths).astype(jnp.int32)


def draw_target_enc(key, part):
    first, second, third = jax.random.split(jax.random.fold_in(key, 303), 3)
    rows = jnp.exp(jax.random.uniform(second, (TOKENS, 1)) * math.log(10.0))
    cols = jnp.exp(jax.random.uniform(third, (1, D)) * math.log(10.0))
    base = jnp.clip(jax.random.normal(first, (TOKENS, D)), -6.0, 6.0)
    return (base * rows * cols).astype(jnp.bfloat16)


def draw_source_enc(key, part):
    first, second, third = jax.random.split(jax.random.fold_in(key, 505), 3)
    rows = jnp.exp(jax.random.uniform(second, (SOURCES, TOKENS, 1)) * math.log(10.0))
    cols = jnp.exp(jax.random.uniform(third, (1, 1, D)) * math.log(10.0))
    base = jnp.clip(jax.random.normal(first, (SOURCES, TOKENS, D)), -6.0, 6.0)
    return (base * rows * cols).astype(jnp.bfloat16)


def draw_queries(key, part):
    first = jax.random.fold_in(jax.random.fold_in(key, 606), 0)
    base = jnp.clip(jax.random.normal(first, (LAYERS, QB, HD)), -6.0, 6.0) * 0.125
    return base.astype(jnp.bfloat16)


def plant(entries, rng, low, high):
    extent = entries.shape
    place = [jax.random.randint(jax.random.fold_in(rng, axis), (), 0, extent[axis]) for axis in range(len(extent))]
    entries = entries.at[tuple(place)].set(low)
    longest = extent.index(max(extent))
    place[longest] = (place[longest] + 1) % extent[longest]
    return entries.at[tuple(place)].set(high)


def shard_levels(key, shape, cuts, least, largest):
    loudness = 1.0
    for position, blocks in cuts:
        steps = jax.random.uniform(jax.random.fold_in(jax.random.fold_in(key, 6), position), (blocks,), jnp.float32, least / len(cuts), largest / len(cuts))
        loudness = loudness * jnp.repeat(jnp.exp(steps), shape[position] // blocks).reshape((-1,) + (1,) * (len(shape) - 1 - position))
    return loudness


def centred(key, dims, deviation, bound, pieces=(), kind=jnp.bfloat16):
    level = shard_levels(key, dims, pieces, -0.22, 0.18) if pieces else 1.0
    result = jax.random.normal(key, dims, jnp.float32) * deviation * level
    return jnp.minimum(jnp.maximum(result, -bound), bound).astype(kind)


def setup_inputs(seed: int = 0) -> dict:
    arg_keys = jax.random.split(jax.random.key(seed), 11)
    return {
        "target_enc": draw_target_enc(jax.random.fold_in(arg_keys[10], 71), 0),
        "source_enc": draw_source_enc(jax.random.fold_in(arg_keys[10], 71), 0),
        "span_start": draw_span_start(jax.random.fold_in(arg_keys[10], 71), 0),
        "span_end": draw_span_end(jax.random.fold_in(arg_keys[10], 71), 0),
        "span_source": plant(jax.random.randint(arg_keys[4], (SPANS,), 0, SOURCES), jax.random.fold_in(arg_keys[4], 1), 0, SOURCES - 1).astype(jnp.int32),
        "norm_gain": jnp.clip(1.0 + 0.18 * jax.random.normal(arg_keys[5], (D,), jnp.float32), 0.1, 1.9),
        "w_key": centred(arg_keys[6], (LAYERS, D, HD), D ** -0.5, 0.09375, ((0, 4), (2, 8))),
        "w_value": centred(arg_keys[7], (LAYERS, D, HD), D ** -0.5, 0.09375, ((0, 4), (2, 8))),
        "queries": draw_queries(jax.random.fold_in(arg_keys[10], 71), 0),
        "key_len": draw_key_len(jax.random.fold_in(arg_keys[10], 71), 0),
    }


def reference(target_enc, source_enc, span_start, span_end, span_source, norm_gain, w_key, w_value, queries, key_len):
    pos = jnp.arange(TOKENS, dtype=jnp.int32)
    covered = (pos[None, :] >= span_start[:, None]) & (pos[None, :] < span_end[:, None])
    which = lax.optimization_barrier(jnp.sum(jnp.where(covered, span_source[:, None], 0), axis=0)).astype(jnp.int32)
    hit = jnp.any(covered, axis=0)
    picked = source_enc[which, pos]
    patched = jnp.where(hit[:, None], picked, target_enc)
    states = patched.astype(jnp.float32)
    meansq = lax.optimization_barrier(jnp.mean(states * states, axis=-1, keepdims=True))
    normed = (states * lax.rsqrt(meansq + 1e-06) * norm_gain).astype(jnp.bfloat16)
    keymask = pos[None, :] < key_len[:, None]

    def one_layer(operands):
        wk, wv, query = operands
        keys = jnp.dot(normed, wk, preferred_element_type=jnp.float32).astype(jnp.bfloat16).reshape(TOKENS, HEADS, HEAD)
        values = jnp.dot(normed, wv, preferred_element_type=jnp.float32).astype(jnp.bfloat16).reshape(TOKENS, HEADS, HEAD)
        qheads = query.reshape(QB, HEADS, HEAD)
        scores = jnp.einsum('qhe,khe->hqk', qheads.astype(jnp.float32), keys.astype(jnp.float32))
        scores = jnp.where(keymask[None], scores, -1e+30)
        top = lax.optimization_barrier(jnp.max(scores, axis=-1, keepdims=True))
        expo = jnp.exp(scores - top)
        probs = (expo / lax.optimization_barrier(jnp.sum(expo, axis=-1, keepdims=True))).astype(jnp.bfloat16)
        mixed = jnp.einsum('hqk,khe->qhe', probs.astype(jnp.float32), values.astype(jnp.float32))
        return mixed.astype(jnp.bfloat16).reshape(QB, HEADS * HEAD)
    return lax.map(one_layer, (w_key, w_value, queries))
```

```python
import functools

import jax
import jax.numpy as jnp
from jax import lax
from jax.experimental import pallas as pl
from jax.experimental.pallas import tpu as pltpu
from jax.sharding import PartitionSpec as P

MESH = pl.DeviceIdType.MESH
CH = 16
QBLK = 128


def kernel(
    S,
    L,
    start_ref,
    end_ref,
    which_ref,
    gain_ref,
    klen_ref,
    target_ref,
    source_ref,
    wk_ref,
    wv_ref,
    q_ref,
    out_ref,
    tgt,
    src,
    merged,
    owner,
    na,
    w,
    q,
    kv,
    scores,
    klen,
    local_sem,
    zs,
    zr,
    rs,
    rr,
    bs,
    br,
):
    rows, D = target_ref.shape
    C = rows // CH
    n = S // 2
    H = n // 2
    T = S * rows
    GR = S * CH
    spans = start_ref.shape[0]
    seglen = T // spans
    here = rows // seglen
    nq = q.shape[0]
    hd = q.shape[1]

    s = lax.axis_index("seq")
    z = lax.axis_index("layer")
    chip = s // 2
    core = s % 2
    sib = chip * 2 + (1 - core)

    def swap(p):
        up = (2 * p) // n
        return p * (1 - up) + up * (3 * n // 2 - 1 - p)

    pos = swap(chip)

    def seq_of(p):
        return swap((p + 2 * n) % n) * 2 + core

    nbr = (seq_of(pos + 1), seq_of(pos - 1))

    local = [
        pltpu.make_async_copy(source_ref.at[0], src, local_sem.at[0]),
        pltpu.make_async_copy(target_ref, tgt, local_sem.at[1]),
        pltpu.make_async_copy(wk_ref.at[0], w.at[0], local_sem.at[2]),
        pltpu.make_async_copy(wv_ref.at[0], w.at[1], local_sem.at[3]),
        pltpu.make_async_copy(q_ref.at[0], q, local_sem.at[4]),
    ]
    for copy in local:
        copy.start()

    barrier = pltpu.get_barrier_semaphore()
    for other in (
        {"seq": nbr[0]},
        {"seq": nbr[1]},
        {"seq": sib},
        {"layer": (z + 1) % L},
        {"layer": (z + L - 1) % L},
    ):
        pl.semaphore_signal(barrier, inc=1, device_id=other, device_id_type=MESH)
    pl.semaphore_wait(barrier, 5)

    def at_rows(c):
        return pl.ds(pl.multiple_of(c * CH, CH), CH)

    def z_copy(d, c, from_input=False):
        source = source_ref.at[0, at_rows(c)] if from_input else merged.at[d, at_rows(c)]
        return pltpu.make_async_remote_copy(
            src_ref=source,
            dst_ref=merged.at[d, at_rows(c)],
            send_sem=zs.at[d, c],
            recv_sem=zr.at[d, c],
            device_id={"layer": (z + 1 - 2 * d + L) % L},
            device_id_type=MESH,
        )

    def ring_copy(d, hop, c):
        origin = seq_of(pos + (-hop if d == 0 else hop))
        return pltpu.make_async_remote_copy(
            src_ref=na.at[origin, at_rows(c)],
            dst_ref=na.at[origin, at_rows(c)],
            send_sem=rs.at[d, hop, c],
            recv_sem=rr.at[d, hop, c],
            device_id={"seq": nbr[d]},
            device_id_type=MESH,
        )

    def sib_copy(rel, c):
        origin = seq_of(pos - rel)
        return pltpu.make_async_remote_copy(
            src_ref=na.at[origin, at_rows(c)],
            dst_ref=na.at[origin, at_rows(c)],
            send_sem=bs.at[rel, c],
            recv_sem=br.at[rel, c],
            device_id={"seq": sib},
            device_id_type=MESH,
        )

    @pl.when(z == 0)
    def _():
        @pl.loop(0, C)
        def _(c):
            z_copy(0, c, True).start()

    @pl.when(z == L - 1)
    def _():
        @pl.loop(0, C)
        def _(c):
            z_copy(1, c, True).start()

    row = s * rows + lax.broadcasted_iota(jnp.int32, (rows, 128), 0)
    own = jnp.full((rows, 128), -1, jnp.int32)
    for k in range(here):
        at = s * here + k
        inside = (row >= start_ref[at]) & (row < end_ref[at])
        own = jnp.where(inside, which_ref[at], own)
    owner[...] = own
    klen[...] = jnp.broadcast_to(klen_ref[...], (128, nq)).T

    local[0].wait()
    local[1].wait()

    def ownership(c):
        return jnp.broadcast_to(owner[at_rows(c), :1], (CH, D))

    def chain(d, c):
        behind = z * (1 - d) + d * (L - 1 - z)
        ahead = z * d + (1 - d) * (L - 1 - z)

        @pl.when(behind > 0)
        def _():
            z_copy(d, c).wait_recv()

            @pl.when(ahead > 0)
            def _():
                mine = src[at_rows(c), :].astype(jnp.float32)
                other = merged[d, at_rows(c), :].astype(jnp.float32)
                merged[d, at_rows(c), :] = jnp.where(ownership(c) == z, mine, other).astype(jnp.bfloat16)
                z_copy(d, c).start()

    first = (2 * z) // L

    def normalize(c):
        who = ownership(c)
        before = merged[0, at_rows(c), :].astype(jnp.float32)
        after = merged[1, at_rows(c), :].astype(jnp.float32)
        states = jnp.where(who < z, before, after)
        states = jnp.where(who == z, src[at_rows(c), :].astype(jnp.float32), states)
        states = jnp.where(who < 0, tgt[at_rows(c), :].astype(jnp.float32), states)
        meansq = jnp.mean(states * states, axis=-1, keepdims=True)
        na[s, at_rows(c), :] = (states * lax.rsqrt(meansq + 1e-06) * gain_ref[...]).astype(jnp.bfloat16)

    def project(c):
        x = na[:, at_rows(c), :].reshape(GR, D)
        keys = jnp.dot(x, w[0], preferred_element_type=jnp.float32).astype(jnp.bfloat16)
        values = jnp.dot(x, w[1], preferred_element_type=jnp.float32).astype(jnp.bfloat16)
        kv[pl.ds(pl.multiple_of(c * GR, GR), GR), :] = values
        scores[:, pl.ds(pl.multiple_of(c * GR, GR), GR)] = lax.dot_general(
            q[...], keys, (((1,), (1,)), ((), ())), preferred_element_type=jnp.float32
        )

    chain(first, 0)

    @pl.loop(0, C + H + 1)
    def _(i):
        @pl.when(i + 1 < C)
        def _():
            chain(first, i + 1)

        @pl.when(i < C)
        def _():
            chain(1 - first, i)
            normalize(i)
            ring_copy(0, 0, i).start()
            ring_copy(1, 0, i).start()
            sib_copy(0, i).start()

        for h in range(1, H + 1):
            c = i - h

            @pl.when((c >= 0) & (c < C))
            def _():
                for d in (0, 1):

                    def arrived(d=d):
                        ring_copy(d, h - 1, c).wait_recv()
                        if h + 1 < H:
                            ring_copy(d, h, c).start()
                        elif h + 1 == H:

                            @pl.when(c % 2 == d)
                            def _():
                                ring_copy(d, h, c).start()

                        sib_copy(h if d == 0 else n - h, c).start()

                    if h < H:
                        arrived()
                    else:
                        pl.when(c % 2 == d)(arrived)

        c = i - H - 1

        @pl.when(c >= 0)
        def _():
            @pl.when(c == 0)
            def _():
                for copy in local[2:]:
                    copy.wait()

            for rel in range(n):
                sib_copy(rel, c).wait_recv()
            project(c)

    col = lax.broadcasted_iota(jnp.int32, (QBLK, T), 1)
    token = (col % GR) // CH * rows + col // GR * CH + col % CH

    @pl.loop(0, nq // QBLK)
    def _(b):
        at = pl.ds(pl.multiple_of(b * QBLK, QBLK), QBLK)
        seen = token < jnp.broadcast_to(klen[at, :1], (QBLK, T))
        sc = jnp.where(seen, scores[at, :], -1e30)
        expo = jnp.exp(sc - jnp.max(sc, axis=-1, keepdims=True))
        probs = (expo * (1.0 / jnp.sum(expo, axis=-1, keepdims=True))).astype(jnp.bfloat16)
        out_ref[0, at, :] = jnp.dot(probs, kv[...], preferred_element_type=jnp.float32).astype(jnp.bfloat16)

    @pl.loop(0, C)
    def _(c):
        @pl.when(z < L - 1)
        def _():
            z_copy(0, c).wait_send()

        @pl.when(z > 0)
        def _():
            z_copy(1, c).wait_send()

        for d in (0, 1):
            for hop in range(H - 1):
                ring_copy(d, hop, c).wait_send()

            @pl.when(c % 2 == d)
            def _():
                ring_copy(d, H - 1, c).wait_send()

        for rel in range(n):
            sib_copy(rel, c).wait_send()


def per_device(
    S,
    L,
    target_enc,
    source_enc,
    span_start,
    span_end,
    span_source,
    norm_gain,
    w_key,
    w_value,
    queries,
    key_len,
):
    rows, D = target_enc.shape
    width = w_key.shape[2]
    nq = queries.shape[1]
    T = S * rows
    C = rows // CH
    n = S // 2
    smem = pl.BlockSpec(memory_space=pltpu.SMEM)
    vmem = pl.BlockSpec(memory_space=pltpu.VMEM)
    anywhere = pl.BlockSpec(memory_space=pl.ANY)
    bf16 = jnp.bfloat16
    return pl.pallas_call(
        functools.partial(kernel, S, L),
        out_shape=jax.ShapeDtypeStruct((1, nq, width), bf16),
        in_specs=[smem, smem, smem, vmem, vmem, anywhere, anywhere, anywhere, anywhere, anywhere],
        out_specs=vmem,
        scratch_shapes=[
            pltpu.VMEM((rows, D), bf16),
            pltpu.VMEM((rows, D), bf16),
            pltpu.VMEM((2, rows, D), bf16),
            pltpu.VMEM((rows, 128), jnp.int32),
            pltpu.VMEM((S, rows, D), bf16),
            pltpu.VMEM((2, D, width), bf16),
            pltpu.VMEM((nq, width), bf16),
            pltpu.VMEM((T, width), bf16),
            pltpu.VMEM((nq, T), jnp.float32),
            pltpu.VMEM((nq, 128), jnp.int32),
            pltpu.SemaphoreType.DMA((5,)),
            pltpu.SemaphoreType.DMA((2, C)),
            pltpu.SemaphoreType.DMA((2, C)),
            pltpu.SemaphoreType.DMA((2, n // 2, C)),
            pltpu.SemaphoreType.DMA((2, n // 2, C)),
            pltpu.SemaphoreType.DMA((n, C)),
            pltpu.SemaphoreType.DMA((n, C)),
        ],
        compiler_params=pltpu.CompilerParams(
            collective_id=0, has_side_effects=True, vmem_limit_bytes=56 << 20
        ),
    )(
        span_start,
        span_end,
        span_source,
        norm_gain.reshape(1, D),
        key_len.reshape(1, nq),
        target_enc,
        source_enc,
        w_key,
        w_value,
        queries,
    )


def solution(mesh):
    return jax.shard_map(
        functools.partial(per_device, mesh.shape["seq"], mesh.shape["layer"]),
        mesh=mesh,
        in_specs=(
            P("seq", None),
            P("layer", "seq", None),
            P(),
            P(),
            P(),
            P(),
            P("layer", None, "seq"),
            P("layer", None, "seq"),
            P("layer", None, "seq"),
            P(),
        ),
        out_specs=P("layer", None, "seq"),
        check_vma=False,
    )
```

```python
import functools

import jax
import jax.numpy as jnp
from jax import lax
from jax.experimental import pallas as pl
from jax.experimental.pallas import tpu as pltpu
from jax.sharding import PartitionSpec as P

MESH = pl.DeviceIdType.MESH
CH = 16
PIECES = 2
AHEAD = 3
QBLK = 128


def kernel(
    S,
    L,
    start_ref,
    end_ref,
    which_ref,
    gain_ref,
    klen_ref,
    target_ref,
    source_ref,
    wk_ref,
    wv_ref,
    q_ref,
    out_ref,
    tgt,
    src,
    merged,
    owner,
    na,
    w,
    q,
    kv,
    scores,
    klen,
    local_sem,
    zs,
    zr,
    rs,
    rr,
    bs,
    br,
):
    rows, D = target_ref.shape
    C = rows // CH
    n = S // 2
    H = n // 2
    T = S * rows
    GR = S * CH
    spans = start_ref.shape[0]
    seglen = T // spans
    here = rows // seglen
    nq = q.shape[0]
    hd = q.shape[1]

    s = lax.axis_index("seq")
    z = lax.axis_index("layer")
    chip = s // 2
    core = s % 2
    sib = chip * 2 + (1 - core)

    def swap(p):
        up = (2 * p) // n
        return p * (1 - up) + up * (3 * n // 2 - 1 - p)

    pos = swap(chip)

    def seq_of(p):
        return swap((p + 2 * n) % n) * 2 + core

    nbr = (seq_of(pos + 1), seq_of(pos - 1))

    local = [
        pltpu.make_async_copy(source_ref.at[0], src, local_sem.at[0]),
        pltpu.make_async_copy(target_ref, tgt, local_sem.at[1]),
        pltpu.make_async_copy(wk_ref.at[0], w.at[0], local_sem.at[2]),
        pltpu.make_async_copy(wv_ref.at[0], w.at[1], local_sem.at[3]),
        pltpu.make_async_copy(q_ref.at[0], q, local_sem.at[4]),
    ]
    for copy in local:
        copy.start()

    barrier = pltpu.get_barrier_semaphore()
    for other in (
        {"seq": nbr[0]},
        {"seq": nbr[1]},
        {"seq": sib},
        {"layer": (z + 1) % L},
        {"layer": (z + L - 1) % L},
    ):
        pl.semaphore_signal(barrier, inc=1, device_id=other, device_id_type=MESH)
    pl.semaphore_wait(barrier, 5)

    def at_rows(c):
        return pl.ds(pl.multiple_of(c * CH, CH), CH)

    def z_copy(d, c, p, from_input=False):
        cols = pl.ds(p * (D // PIECES), D // PIECES)
        source = source_ref.at[0, at_rows(c), cols] if from_input else merged.at[d, at_rows(c), cols]
        return pltpu.make_async_remote_copy(
            src_ref=source,
            dst_ref=merged.at[d, at_rows(c), cols],
            send_sem=zs.at[d, c, p],
            recv_sem=zr.at[d, c, p],
            device_id={"layer": (z + 1 - 2 * d + L) % L},
            device_id_type=MESH,
        )

    def ring_copy(d, hop, c):
        origin = seq_of(pos + (-hop if d == 0 else hop))
        cols = pl.ds(d * (D // 2), D // 2) if hop == H - 1 else pl.ds(0, D)
        return pltpu.make_async_remote_copy(
            src_ref=na.at[origin, at_rows(c), cols],
            dst_ref=na.at[origin, at_rows(c), cols],
            send_sem=rs.at[d, hop, c],
            recv_sem=rr.at[d, hop, c],
            device_id={"seq": nbr[d]},
            device_id_type=MESH,
        )

    def sib_copy(rel, c):
        origin = seq_of(pos - (H if rel == n else rel))
        cols = pl.ds((rel // n) * (D // 2), D // 2) if rel in (H, n) else pl.ds(0, D)
        return pltpu.make_async_remote_copy(
            src_ref=na.at[origin, at_rows(c), cols],
            dst_ref=na.at[origin, at_rows(c), cols],
            send_sem=bs.at[rel, c],
            recv_sem=br.at[rel, c],
            device_id={"seq": sib},
            device_id_type=MESH,
        )

    @pl.when(z == 0)
    def _():
        @pl.loop(0, C)
        def _(c):
            for p in range(PIECES):
                z_copy(0, c, p, True).start()

    @pl.when(z == L - 1)
    def _():
        @pl.loop(0, C)
        def _(c):
            for p in range(PIECES):
                z_copy(1, c, p, True).start()

    row = s * rows + lax.broadcasted_iota(jnp.int32, (rows, 128), 0)
    own = jnp.full((rows, 128), -1, jnp.int32)
    for k in range(here):
        at = s * here + k
        inside = (row >= start_ref[at]) & (row < end_ref[at])
        own = jnp.where(inside, which_ref[at], own)
    owner[...] = own
    klen[...] = jnp.broadcast_to(klen_ref[...], (128, nq)).T

    local[0].wait()
    local[1].wait()

    def ownership(c):
        return jnp.broadcast_to(owner[at_rows(c), :1], (CH, D))

    def chain(d, c):
        behind = z * (1 - d) + d * (L - 1 - z)
        ahead = z * d + (1 - d) * (L - 1 - z)

        @pl.when((behind > 0) & (ahead > 0))
        def _():
            who = jnp.broadcast_to(owner[at_rows(c), :1], (CH, D // PIECES))
            for p in range(PIECES):
                cols = pl.ds(p * (D // PIECES), D // PIECES)
                z_copy(d, c, p).wait_recv()
                mine = src[at_rows(c), cols].astype(jnp.float32)
                other = merged[d, at_rows(c), cols].astype(jnp.float32)
                merged[d, at_rows(c), cols] = jnp.where(who == z, mine, other).astype(jnp.bfloat16)
                z_copy(d, c, p).start()

        @pl.when((behind > 0) & (ahead == 0))
        def _():
            for p in range(PIECES):
                z_copy(d, c, p).wait_recv()

    first = (2 * z) // L

    def normalize(c):
        who = ownership(c)
        before = merged[0, at_rows(c), :].astype(jnp.float32)
        after = merged[1, at_rows(c), :].astype(jnp.float32)
        states = jnp.where(who < z, before, after)
        states = jnp.where(who == z, src[at_rows(c), :].astype(jnp.float32), states)
        states = jnp.where(who < 0, tgt[at_rows(c), :].astype(jnp.float32), states)
        meansq = jnp.mean(states * states, axis=-1, keepdims=True)
        na[s, at_rows(c), :] = (states * lax.rsqrt(meansq + 1e-06) * gain_ref[...]).astype(jnp.bfloat16)

    def project(c):
        x = na[:, at_rows(c), :].reshape(GR, D)
        keys = jnp.dot(x, w[0], preferred_element_type=jnp.float32).astype(jnp.bfloat16)
        values = jnp.dot(x, w[1], preferred_element_type=jnp.float32).astype(jnp.bfloat16)
        kv[pl.ds(pl.multiple_of(c * GR, GR), GR), :] = values
        scores[:, pl.ds(pl.multiple_of(c * GR, GR), GR)] = lax.dot_general(
            q[...], keys, (((1,), (1,)), ((), ())), preferred_element_type=jnp.float32
        )

    middle = (z > 0) & (z < L - 1)

    @pl.when(middle)
    def _():
        for k in range(min(AHEAD, C)):
            chain(first, k)
            if k > 0:
                chain(1 - first, k - 1)

    @pl.loop(0, C + H + 1)
    def _(i):
        @pl.when(middle & (i + AHEAD < C))
        def _():
            chain(first, i + AHEAD)

        @pl.when(middle & (i + AHEAD - 1 < C))
        def _():
            chain(1 - first, i + AHEAD - 1)

        @pl.when(i < C)
        def _():
            @pl.when(jnp.logical_not(middle))
            def _():
                chain(1 - first, i)

            normalize(i)
            ring_copy(0, 0, i).start()
            ring_copy(1, 0, i).start()
            sib_copy(0, i).start()

        for h in range(1, H + 1):
            c = i - h

            @pl.when((c >= 0) & (c < C))
            def _():
                for d in (0, 1):
                    ring_copy(d, h - 1, c).wait_recv()
                    if h < H:
                        ring_copy(d, h, c).start()
                for d in (0, 1):
                    sib_copy(h if d == 0 else (n if h == H else n - h), c).start()

        c = i - H - 1

        @pl.when(c >= 0)
        def _():
            @pl.when(c == 0)
            def _():
                for copy in local[2:]:
                    copy.wait()

            for rel in range(n + 1):
                sib_copy(rel, c).wait_recv()
            project(c)

    col = lax.broadcasted_iota(jnp.int32, (QBLK, T), 1)
    token = (col % GR) // CH * rows + col // GR * CH + col % CH

    @pl.loop(0, nq // QBLK)
    def _(b):
        at = pl.ds(pl.multiple_of(b * QBLK, QBLK), QBLK)
        seen = token < jnp.broadcast_to(klen[at, :1], (QBLK, T))
        sc = jnp.where(seen, scores[at, :], -1e30)
        expo = jnp.exp(sc - jnp.max(sc, axis=-1, keepdims=True))
        probs = (expo * (1.0 / jnp.sum(expo, axis=-1, keepdims=True))).astype(jnp.bfloat16)
        out_ref[0, at, :] = jnp.dot(probs, kv[...], preferred_element_type=jnp.float32).astype(jnp.bfloat16)

    @pl.loop(0, C)
    def _(c):
        @pl.when(z < L - 1)
        def _():
            for p in range(PIECES):
                z_copy(0, c, p).wait_send()

        @pl.when(z > 0)
        def _():
            for p in range(PIECES):
                z_copy(1, c, p).wait_send()

        for d in (0, 1):
            for hop in range(H):
                ring_copy(d, hop, c).wait_send()

        for rel in range(n + 1):
            sib_copy(rel, c).wait_send()


def per_device(
    S,
    L,
    target_enc,
    source_enc,
    span_start,
    span_end,
    span_source,
    norm_gain,
    w_key,
    w_value,
    queries,
    key_len,
):
    rows, D = target_enc.shape
    width = w_key.shape[2]
    nq = queries.shape[1]
    T = S * rows
    C = rows // CH
    n = S // 2
    smem = pl.BlockSpec(memory_space=pltpu.SMEM)
    vmem = pl.BlockSpec(memory_space=pltpu.VMEM)
    anywhere = pl.BlockSpec(memory_space=pl.ANY)
    bf16 = jnp.bfloat16
    return pl.pallas_call(
        functools.partial(kernel, S, L),
        out_shape=jax.ShapeDtypeStruct((1, nq, width), bf16),
        in_specs=[smem, smem, smem, vmem, vmem, anywhere, anywhere, anywhere, anywhere, anywhere],
        out_specs=vmem,
        scratch_shapes=[
            pltpu.VMEM((rows, D), bf16),
            pltpu.VMEM((rows, D), bf16),
            pltpu.VMEM((2, rows, D), bf16),
            pltpu.VMEM((rows, 128), jnp.int32),
            pltpu.VMEM((S, rows, D), bf16),
            pltpu.VMEM((2, D, width), bf16),
            pltpu.VMEM((nq, width), bf16),
            pltpu.VMEM((T, width), bf16),
            pltpu.VMEM((nq, T), jnp.float32),
            pltpu.VMEM((nq, 128), jnp.int32),
            pltpu.SemaphoreType.DMA((5,)),
            pltpu.SemaphoreType.DMA((2, C, PIECES)),
            pltpu.SemaphoreType.DMA((2, C, PIECES)),
            pltpu.SemaphoreType.DMA((2, n // 2, C)),
            pltpu.SemaphoreType.DMA((2, n // 2, C)),
            pltpu.SemaphoreType.DMA((n + 1, C)),
            pltpu.SemaphoreType.DMA((n + 1, C)),
        ],
        compiler_params=pltpu.CompilerParams(
            collective_id=0, has_side_effects=True, vmem_limit_bytes=56 << 20
        ),
    )(
        span_start,
        span_end,
        span_source,
        norm_gain.reshape(1, D),
        key_len.reshape(1, nq),
        target_enc,
        source_enc,
        w_key,
        w_value,
        queries,
    )


def solution(mesh):
    return jax.shard_map(
        functools.partial(per_device, mesh.shape["seq"], mesh.shape["layer"]),
        mesh=mesh,
        in_specs=(
            P("seq", None),
            P("layer", "seq", None),
            P(),
            P(),
            P(),
            P(),
            P("layer", None, "seq"),
            P("layer", None, "seq"),
            P("layer", None, "seq"),
            P(),
        ),
        out_specs=P("layer", None, "seq"),
        check_vma=False,
    )
```

```python
import functools

import jax
import jax.numpy as jnp
from jax import lax
from jax.experimental import pallas as pl
from jax.experimental.pallas import tpu as pltpu
from jax.sharding import PartitionSpec as P

MESH = pl.DeviceIdType.MESH
CH = 16
PIECES = 2
AHEAD = 2
SKEW = 3
QBLK = 512


def kernel(
    S,
    L,
    start_ref,
    end_ref,
    which_ref,
    gain_ref,
    klen_ref,
    target_ref,
    source_ref,
    wk_ref,
    wv_ref,
    q_ref,
    out_ref,
    tgt,
    src,
    merged,
    owner,
    na,
    w,
    q,
    kv,
    scores,
    klen,
    local_sem,
    zs,
    zr,
    rs,
    rr,
    bs,
    br,
):
    rows, D = target_ref.shape
    C = rows // CH
    n = S // 2
    H = n // 2
    T = S * rows
    GR = S * CH
    spans = start_ref.shape[0]
    seglen = T // spans
    here = rows // seglen
    nq = q.shape[0]
    hd = q.shape[1]

    s = lax.axis_index("seq")
    z = lax.axis_index("layer")
    chip = s // 2
    core = s % 2
    sib = chip * 2 + (1 - core)

    def swap(p):
        up = (2 * p) // n
        return p * (1 - up) + up * (3 * n // 2 - 1 - p)

    pos = swap(chip)

    def seq_of(p):
        return swap((p + 2 * n) % n) * 2 + core

    nbr = (seq_of(pos + 1), seq_of(pos - 1))

    local = [
        pltpu.make_async_copy(source_ref.at[0], src, local_sem.at[0]),
        pltpu.make_async_copy(target_ref, tgt, local_sem.at[1]),
        pltpu.make_async_copy(wk_ref.at[0], w.at[0], local_sem.at[2]),
        pltpu.make_async_copy(wv_ref.at[0], w.at[1], local_sem.at[3]),
        pltpu.make_async_copy(q_ref.at[0], q, local_sem.at[4]),
    ]
    for copy in local:
        copy.start()

    barrier = pltpu.get_barrier_semaphore()
    for other in (
        {"seq": nbr[0]},
        {"seq": nbr[1]},
        {"seq": sib},
        {"layer": (z + 1) % L},
        {"layer": (z + L - 1) % L},
    ):
        pl.semaphore_signal(barrier, inc=1, device_id=other, device_id_type=MESH)
    pl.semaphore_wait(barrier, 5)

    def at_rows(c):
        if c is None:
            return pl.ds(0, rows)
        return pl.ds(pl.multiple_of(c * CH, CH), CH)

    def z_copy(d, c, p, from_input=False):
        cols = pl.ds(0, D) if p is None else pl.ds(p * (D // PIECES), D // PIECES)
        source = source_ref.at[0, at_rows(c), cols] if from_input else merged.at[d, at_rows(c), cols]
        return pltpu.make_async_remote_copy(
            src_ref=source,
            dst_ref=merged.at[d, at_rows(c), cols],
            send_sem=zs.at[d],
            recv_sem=zr.at[d, 0 if c is None else c, 0 if p is None else p],
            device_id={"layer": (z + 1 - 2 * d + L) % L},
            device_id_type=MESH,
        )

    def ring_copy(d, hop, c):
        origin = seq_of(pos + (-hop if d == 0 else hop))
        cols = pl.ds(d * (D // 2), D // 2) if hop == H - 1 else pl.ds(0, D)
        return pltpu.make_async_remote_copy(
            src_ref=na.at[origin, at_rows(c), cols],
            dst_ref=na.at[origin, at_rows(c), cols],
            send_sem=rs.at[d, hop],
            recv_sem=rr.at[d, hop, 0 if c is None else c],
            device_id={"seq": nbr[d]},
            device_id_type=MESH,
        )

    def sib_copy(rel, c):
        origin = seq_of(pos - (H if rel == n else rel))
        cols = pl.ds((rel // n) * (D // 2), D // 2) if rel in (H, n) else pl.ds(0, D)
        return pltpu.make_async_remote_copy(
            src_ref=na.at[origin, at_rows(c), cols],
            dst_ref=na.at[origin, at_rows(c), cols],
            send_sem=bs.at[rel],
            recv_sem=br.at[rel, 0 if c is None else c],
            device_id={"seq": sib},
            device_id_type=MESH,
        )

    @pl.when(z == 0)
    def _():
        @pl.loop(0, C)
        def _(c):
            for p in range(PIECES):
                z_copy(0, c, p, True).start()

    @pl.when(z == L - 1)
    def _():
        @pl.loop(0, C)
        def _(c):
            for p in range(PIECES):
                z_copy(1, c, p, True).start()

    row = s * rows + lax.broadcasted_iota(jnp.int32, (rows, 128), 0)
    own = jnp.full((rows, 128), -1, jnp.int32)
    for k in range(here):
        at = s * here + k
        inside = (row >= start_ref[at]) & (row < end_ref[at])
        own = jnp.where(inside, which_ref[at], own)
    owner[...] = own
    klen[...] = jnp.broadcast_to(klen_ref[...], (128, nq)).T

    local[0].wait()
    local[1].wait()

    def ownership(c):
        return jnp.broadcast_to(owner[at_rows(c), :1], (CH, D))

    def chain(d, c):
        behind = z * (1 - d) + d * (L - 1 - z)
        ahead = z * d + (1 - d) * (L - 1 - z)

        @pl.when((behind > 0) & (ahead > 0))
        def _():
            who = jnp.broadcast_to(owner[at_rows(c), :1], (CH, D // PIECES))
            for p in range(PIECES):
                cols = pl.ds(p * (D // PIECES), D // PIECES)
                z_copy(d, c, p).wait_recv()
                mine = src[at_rows(c), cols].astype(jnp.float32)
                other = merged[d, at_rows(c), cols].astype(jnp.float32)
                merged[d, at_rows(c), cols] = jnp.where(who == z, mine, other).astype(jnp.bfloat16)
                z_copy(d, c, p).start()

        @pl.when((behind > 0) & (ahead == 0))
        def _():
            for p in range(PIECES):
                z_copy(d, c, p).wait_recv()

    first = (2 * z) // L

    def normalize(c):
        who = ownership(c)
        before = merged[0, at_rows(c), :].astype(jnp.float32)
        after = merged[1, at_rows(c), :].astype(jnp.float32)
        states = jnp.where(who < z, before, after)
        states = jnp.where(who == z, src[at_rows(c), :].astype(jnp.float32), states)
        states = jnp.where(who < 0, tgt[at_rows(c), :].astype(jnp.float32), states)
        meansq = jnp.mean(states * states, axis=-1, keepdims=True)
        na[s, at_rows(c), :] = (states * lax.rsqrt(meansq + 1e-06) * gain_ref[...]).astype(jnp.bfloat16)

    def project(c):
        x = na[:, at_rows(c), :].reshape(GR, D)
        keys = jnp.dot(x, w[0], preferred_element_type=jnp.float32).astype(jnp.bfloat16)
        values = jnp.dot(x, w[1], preferred_element_type=jnp.float32).astype(jnp.bfloat16)
        kv[pl.ds(pl.multiple_of(c * GR, GR), GR), :] = values
        scores[:, pl.ds(pl.multiple_of(c * GR, GR), GR)] = lax.dot_general(
            q[...], keys, (((1,), (1,)), ((), ())), preferred_element_type=jnp.float32
        )

    middle = (z > 0) & (z < L - 1)

    @pl.when(middle)
    def _():
        for k in range(min(AHEAD, C)):
            chain(first, k)
            if k > 0:
                chain(1 - first, k - 1)

    @pl.loop(0, C + SKEW * H + 1)
    def _(i):
        @pl.when(middle & (i + AHEAD < C))
        def _():
            chain(first, i + AHEAD)

        @pl.when(middle & (i + AHEAD - 1 < C))
        def _():
            chain(1 - first, i + AHEAD - 1)

        @pl.when(i < C)
        def _():
            @pl.when(jnp.logical_not(middle))
            def _():
                chain(1 - first, i)

            normalize(i)
            ring_copy(0, 0, i).start()
            ring_copy(1, 0, i).start()
            sib_copy(0, i).start()

        for h in range(1, H + 1):
            c = i - SKEW * h

            @pl.when((c >= 0) & (c < C))
            def _():
                for d in (0, 1):
                    ring_copy(d, h - 1, c).wait_recv()
                    if h < H:
                        ring_copy(d, h, c).start()
                for d in (0, 1):
                    sib_copy(h if d == 0 else (n if h == H else n - h), c).start()

        c = i - SKEW * H - 1

        @pl.when(c >= 0)
        def _():
            @pl.when(c == 0)
            def _():
                for copy in local[2:]:
                    copy.wait()

            for rel in range(n + 1):
                sib_copy(rel, c).wait_recv()
            project(c)

    col = lax.broadcasted_iota(jnp.int32, (QBLK, T), 1)
    token = (col % GR) // CH * rows + col // GR * CH + col % CH

    @pl.loop(0, nq // QBLK)
    def _(b):
        at = pl.ds(pl.multiple_of(b * QBLK, QBLK), QBLK)
        seen = token < jnp.broadcast_to(klen[at, :1], (QBLK, T))
        sc = jnp.where(seen, scores[at, :], -1e30)
        expo = jnp.exp(sc - jnp.max(sc, axis=-1, keepdims=True))
        probs = (expo * (1.0 / jnp.sum(expo, axis=-1, keepdims=True))).astype(jnp.bfloat16)
        out_ref[0, at, :] = jnp.dot(probs, kv[...], preferred_element_type=jnp.float32).astype(jnp.bfloat16)

    @pl.when(z < L - 1)
    def _():
        z_copy(0, None, None).wait_send()

    @pl.when(z > 0)
    def _():
        z_copy(1, None, None).wait_send()

    for d in (0, 1):
        for hop in range(H):
            ring_copy(d, hop, None).wait_send()

    for rel in range(n + 1):
        sib_copy(rel, None).wait_send()


def per_device(
    S,
    L,
    target_enc,
    source_enc,
    span_start,
    span_end,
    span_source,
    norm_gain,
    w_key,
    w_value,
    queries,
    key_len,
):
    rows, D = target_enc.shape
    width = w_key.shape[2]
    nq = queries.shape[1]
    T = S * rows
    C = rows // CH
    n = S // 2
    smem = pl.BlockSpec(memory_space=pltpu.SMEM)
    vmem = pl.BlockSpec(memory_space=pltpu.VMEM)
    anywhere = pl.BlockSpec(memory_space=pl.ANY)
    bf16 = jnp.bfloat16
    return pl.pallas_call(
        functools.partial(kernel, S, L),
        out_shape=jax.ShapeDtypeStruct((1, nq, width), bf16),
        in_specs=[smem, smem, smem, vmem, vmem, anywhere, anywhere, anywhere, anywhere, anywhere],
        out_specs=vmem,
        scratch_shapes=[
            pltpu.VMEM((rows, D), bf16),
            pltpu.VMEM((rows, D), bf16),
            pltpu.VMEM((2, rows, D), bf16),
            pltpu.VMEM((rows, 128), jnp.int32),
            pltpu.VMEM((S, rows, D), bf16),
            pltpu.VMEM((2, D, width), bf16),
            pltpu.VMEM((nq, width), bf16),
            pltpu.VMEM((T, width), bf16),
            pltpu.VMEM((nq, T), jnp.float32),
            pltpu.VMEM((nq, 128), jnp.int32),
            pltpu.SemaphoreType.DMA((5,)),
            pltpu.SemaphoreType.DMA((2,)),
            pltpu.SemaphoreType.DMA((2, C, PIECES)),
            pltpu.SemaphoreType.DMA((2, n // 2)),
            pltpu.SemaphoreType.DMA((2, n // 2, C)),
            pltpu.SemaphoreType.DMA((n + 1,)),
            pltpu.SemaphoreType.DMA((n + 1, C)),
        ],
        compiler_params=pltpu.CompilerParams(
            collective_id=0, has_side_effects=True, vmem_limit_bytes=56 << 20
        ),
    )(
        span_start,
        span_end,
        span_source,
        norm_gain.reshape(1, D),
        key_len.reshape(1, nq),
        target_enc,
        source_enc,
        w_key,
        w_value,
        queries,
    )


def solution(mesh):
    return jax.shard_map(
        functools.partial(per_device, mesh.shape["seq"], mesh.shape["layer"]),
        mesh=mesh,
        in_specs=(
            P("seq", None),
            P("layer", "seq", None),
            P(),
            P(),
            P(),
            P(),
            P("layer", None, "seq"),
            P("layer", None, "seq"),
            P("layer", None, "seq"),
            P(),
        ),
        out_specs=P("layer", None, "seq"),
        check_vma=False,
    )
```
